1024 devices in a mesh: section: 2 (over y_hi), dp: 8 (over x, core), expert: 64 (over z, y_lo).
Axes of the slice: x: 4, y: 4 (y_hi: 2, y_lo: 2; y = y_hi * 2 + y_lo), z: 32, core: 2. Of those that a mesh axis runs over, the one named last changes fastest.
Arguments:
- activations: bfloat16 [2, 4096, 4096], P('section', 'expert'), may hold values from -6 to 6
- routes: int32 [2, 4096, 8], P('section', 'expert'), may hold values from 0 to 63, all different within a row; in each aligned block of 64 rows (0 to 63, 64 to 127, ..., all dimensions but the last counted through in order) at most 8 rows name the same one
- gate_weights: float32 [2, 4096, 8], P('section', 'expert'), may hold values from 0.05 to 0.5
- norm_gain: bfloat16 [4096], replicated, may hold values from 0.099609375 to 1.8984375
- gate_up_weights: bfloat16 [64, 2, 1536, 4096], P('expert', None, 'dp'), may hold values from -0.09375 to 0.09375
- down_weights: bfloat16 [64, 1536, 4096], P('expert', None, 'dp'), may hold values from -0.15625 to 0.15625
Outputs:
- arrived: bfloat16 [2, 4096, 4096], P('section', 'expert', 'dp')
The draws below stay inside these ranges and needn't reach their ends.
Inputs may be any that keep to these rules, and one draw needn't show every extreme that they name: `routes`: each token names 8 different experts. Among the 64 tokens of one device (aligned blocks of 64 tokens), no expert is named more than 8 times, and in some blocks one expert is named exactly 8 times.
All inputs are finite; a program needn't handle non-finite values.
Results may differ from the reference program's by a relative error of at most 0.005.
Values may be sent and summed in bfloat16 or wider, within the bound.
A program may use at most 32 MiB of HBM per device.

```python
import math
import jax
import jax.numpy as jnp
import numpy as np
from jax import lax

D = 4096
FF = 1536
TOP = 8
TOK_DEV = 64
EXPERTS = 64
CAP = 8
TOKENS = 4096
N_EXPERT = 64


def levels(key, extent, cuts, least, high):
    loudness = 1.0
    for axis_at, blocks in cuts:
        draws = jax.random.uniform(jax.random.fold_in(jax.random.fold_in(key, 6), axis_at), (blocks,), jnp.float32, least / len(cuts), high / len(cuts))
        loudness = loudness * jnp.repeat(jnp.exp(draws), extent[axis_at] // blocks).reshape((-1,) + (1,) * (len(extent) - 1 - axis_at))
    return loudness


def shared_out(stream_key, own, number, rows, amount, top, limit, skew):
    ranking = jax.random.permutation(stream_key, amount)
    crowded, usual = shares(amount, rows * top, limit, skew, True), shares(amount, rows * top, limit, skew, False)
    places = jnp.arange(amount)

    def named(tallies, turn):
        used = int((tallies > 0).sum())
        fixed = max(1, used // 4)
        passed = fixed + (places - fixed + turn * (used - fixed)) % max(1, amount - fixed)
        return jnp.zeros((amount,), jnp.int32).at[ranking[jnp.where(places < fixed, places, passed)]].set(jnp.asarray(tallies, jnp.int32))

    tallies = jnp.where(number % 4 == 0, named(crowded, number // 4), named(usual, number - number // 4 - 1))
    mixed = jax.random.permutation(jax.random.fold_in(own, 3), amount)
    source_of, taker = mixed[0:amount // 2 * 2:2], mixed[1:amount // 2 * 2:2]
    room = jnp.minimum(tallies[source_of] - 1, limit - tallies[taker]) // 2
    room = jnp.where((source_of == ranking[0]) | (taker == ranking[0]) | (tallies[taker] == 0), 0, jnp.maximum(room, 0))
    passed = jax.random.randint(jax.random.fold_in(own, 4), (amount // 2,), 0, 1 << 20) % (room + 1)
    tallies = tallies.at[source_of].add(-passed).at[taker].add(passed)
    labels = jnp.searchsorted(jnp.cumsum(tallies), jnp.arange(rows * top), side="right").astype(jnp.int32)
    table = labels.reshape(top, rows).T
    table = table[jax.random.permutation(jax.random.fold_in(own, 1), rows)]
    turn = jax.random.randint(jax.random.fold_in(own, 2), (rows, 1), 0, top)
    return jnp.take_along_axis(table, (jnp.arange(top)[None, :] + turn) % top, axis=1)


def shares(amount, total, bound, lean, full):
    loads = [(1 << 20) // math.isqrt(grade ** lean) + 1 for grade in range(1, amount + 1)]
    largest = bound if full else min(bound, max(-(-total // amount), total * loads[0] // sum(loads)))
    least = 1 if total - largest >= amount - 1 else 0
    counts, surplus = [largest] + [least] * (amount - 1), total - largest - least * (amount - 1)
    while surplus > 0:
        movable = [i for i in range(1, amount) if counts[i] < largest] or [i for i in range(1, amount) if counts[i] < bound]
        mass, left = sum([loads[i] for i in movable]), surplus
        for i in movable:
            addition = min(bound - counts[i], max(1, left * loads[i] // mass), surplus)
            counts[i] = counts[i] + addition
            surplus = surplus - addition
    return np.array(counts)


def normal_values(rng, shape, width, bound, pieces=(), kind=jnp.bfloat16):
    level = levels(rng, shape, pieces, -0.22, 0.18) if pieces else 1.0
    result = jax.random.normal(rng, shape, jnp.float32) * width * level
    return jnp.minimum(jnp.maximum(result, -bound), bound).astype(kind)


def setup_inputs(seed: int = 0) -> dict:
    streams_of = jax.random.split(jax.random.key(seed), 7)
    activations = normal_values(streams_of[0], (2, TOKENS, D), 1.0, 6.0, ((0, 2), (1, 64)))
    routes_keys = jax.random.split(jax.random.fold_in(streams_of[1], 1), 2 * TOKENS // TOK_DEV)
    routes_turns = jax.random.permutation(jax.random.fold_in(streams_of[1], 3), 2 * TOKENS // TOK_DEV)
    routes = jax.vmap(lambda own, number: shared_out(jax.random.fold_in(streams_of[1], 2), own, number, TOK_DEV, EXPERTS, TOP, CAP, 2))(routes_keys, routes_turns).reshape((2, TOKENS, TOP))
    gate_weights = jnp.clip(jnp.exp(math.log(0.5) - 2.3025851 * jax.random.uniform(streams_of[2], (2, TOKENS, TOP), jnp.float32) ** levels(streams_of[2], (2, TOKENS, TOP), ((0, 2), (1, 64)), -0.2, 0.2)), 0.05, 0.5)
    norm_gain = jnp.clip(1.0 + 0.18 * jax.random.normal(streams_of[3], (D,), jnp.float32), 0.099609375, 1.8984375).astype(jnp.bfloat16)
    gate_up_weights = normal_values(streams_of[4], (EXPERTS, 2, FF, D), D ** -0.5, 0.09375, ((0, 64), (2, 8)))
    down_weights = normal_values(streams_of[5], (EXPERTS, FF, D), FF ** -0.5, 0.15625, ((0, 64), (2, 8)))
    return dict(activations=activations, routes=routes, gate_weights=gate_weights, norm_gain=norm_gain, gate_up_weights=gate_up_weights, down_weights=down_weights)


def normalize(values, norm_gain):
    widened = values.astype(jnp.float32)
    mean_square = lax.optimization_barrier(jnp.mean(widened * widened, axis=-1, keepdims=True))
    return (widened * lax.rsqrt(mean_square + 1e-06) * norm_gain.astype(jnp.float32)).astype(jnp.bfloat16)

def expert_apply(packed):
    slot_rows, in_weights, out_weights = packed
    contract = (((1,), (1,)), ((), ()))
    gate_val = lax.dot_general(slot_rows, in_weights[0], contract, preferred_element_type=jnp.float32)
    up_val = lax.dot_general(slot_rows, in_weights[1], contract, preferred_element_type=jnp.float32)
    hidden_act = (jax.nn.silu(gate_val) * up_val).astype(jnp.bfloat16)
    return jnp.dot(hidden_act, out_weights, preferred_element_type=jnp.float32).astype(jnp.bfloat16)

def layer_apply(activations, routes, gate_weights, norm_gain, gate_up_weights, down_weights):
    normed = normalize(activations, norm_gain)
    token_count = activations.shape[0]
    flat_routes = routes.reshape(-1).astype(jnp.int32)
    experts_iota = jnp.arange(EXPERTS, dtype=jnp.int32)
    onehot = (flat_routes[:, None] == experts_iota[None, :]).astype(jnp.int32)
    slot_ranks = lax.optimization_barrier(jnp.sum((jnp.cumsum(onehot, axis=0) - onehot) * onehot, axis=1)).astype(jnp.int32)
    owners = jnp.arange(flat_routes.shape[0], dtype=jnp.int32) // TOP
    slot_depth = N_EXPERT * CAP
    buffers = jnp.zeros((EXPERTS, slot_depth, D), jnp.bfloat16).at[flat_routes, slot_ranks].set(normed[owners])
    results = lax.map(expert_apply, (buffers, gate_up_weights, down_weights))
    picked = results[flat_routes, slot_ranks].reshape(token_count, TOP, D).astype(jnp.float32)
    branch = lax.optimization_barrier(jnp.sum(picked * gate_weights.astype(jnp.float32)[:, :, None], axis=1))
    return (activations.astype(jnp.float32) + branch).astype(jnp.bfloat16)

def reference(activations, routes, gate_weights, norm_gain, gate_up_weights, down_weights):
    from_first = layer_apply(activations[0], routes[0], gate_weights[0], norm_gain, gate_up_weights, down_weights)
    second = layer_apply(activations[1], routes[1], gate_weights[1], norm_gain, gate_up_weights, down_weights)
    return jnp.stack([second, from_first])
```

```python
import functools

import jax
import jax.numpy as jnp
from jax import lax
from jax.experimental import pallas as pl
from jax.experimental.pallas import tpu as pltpu
from jax.sharding import PartitionSpec as P

MESH = pl.DeviceIdType.MESH
F32, BF16 = jnp.float32, jnp.bfloat16
CHUNKS = 4
GROUPS = 4


def remote(src, dst, send, recv, device):
    return pltpu.make_async_remote_copy(
        src_ref=src, dst_ref=dst, send_sem=send, recv_sem=recv, device_id=device, device_id_type=MESH
    )


def kernel(
    n_dp, n_exp,
    x_ref, rg_ref, gain_ref, gu_hbm, dn_hbm, out_ref,
    guv, dnv, blk, mt, cw, tri, ys, xg, ab, eo, rr, rbl, rbr, ct, oc, fin,
    load_sem, ring_s, ring_r, meta_s, meta_r, y_s, y_r, x_s, x_r, rel_s, rel_r, pc_s, pc_r,
    ax_s, ax_r, al_s, al_r, ap_s, ap_r, yb_s, yb_r, rs_s, rs_r, fin_s, fin_r,
):
    sec, dp, ex = lax.axis_index("section"), lax.axis_index("dp"), lax.axis_index("expert")
    n_z = n_exp // 2
    half = n_z // 2
    z, yl = ex // 2, lax.rem(ex, 2)
    tokens, width = blk.shape[1], blk.shape[2]
    part = tokens // CHUNKS
    right = (sec, dp, lax.rem(ex + 2, n_exp))
    left = (sec, dp, lax.rem(ex + n_exp - 2, n_exp))
    ynb = (sec, dp, ex + 1 - 2 * yl)
    dp_up, dp_down = lax.rem(dp + 2, n_dp), lax.rem(dp + n_dp - 2, n_dp)
    dp_far = lax.rem(dp + n_dp // 2, n_dp)
    dp_pc = dp + 1 - 2 * lax.rem(dp, 2)
    x_up, x_down, core = (sec, dp_up, ex), (sec, dp_down, ex), (sec, dp_pc, ex)
    over = (1 - sec, dp, ex)

    barrier = pltpu.get_barrier_semaphore()
    for peer in (right, left, ynb, x_up, x_down, core, over):
        pl.semaphore_signal(barrier, inc=1, device_id=peer, device_id_type=MESH)
    load_gu = pltpu.make_async_copy(gu_hbm, guv, load_sem.at[0])
    load_dn = pltpu.make_async_copy(dn_hbm, dnv, load_sem.at[1])
    load_gu.start()
    load_dn.start()

    wide = x_ref[...].astype(F32)
    scale = lax.rsqrt(jnp.mean(wide * wide, axis=-1, keepdims=True) + 1e-06)
    mine = pl.ds(pl.multiple_of(dp * width, width), width)
    blk[z] = (x_ref[:, mine].astype(F32) * scale * gain_ref[:, mine].astype(F32)).astype(BF16)
    mt[z] = rg_ref[...]
    a_tok = lax.broadcasted_iota(jnp.int32, (128, 128), 0)
    b_tok = lax.broadcasted_iota(jnp.int32, (128, 128), 1)
    tri[...] = jnp.where((a_tok < b_tok) & ((a_tok < 64) == (b_tok < 64)), 1.0, 0.0).astype(BF16)
    lane = lax.broadcasted_iota(jnp.int32, (8, 128), 1)
    sub = lax.broadcasted_iota(jnp.int32, (8, 128), 0)
    row16 = lax.broadcasted_iota(jnp.int32, (16, 128), 0).astype(F32)
    ex_own, ex_other = ex.astype(F32), (ex + 1 - 2 * yl).astype(F32)
    pl.semaphore_wait(barrier, 7)

    def ring(flow, k, piece):
        at = lax.rem(z + n_z - k, n_z) if flow == 0 else lax.rem(z + k, n_z)
        ref = blk.at[at, pl.ds(piece * part, part)]
        return ref, at

    def ring_send(flow, k, piece):
        ref, _ = ring(flow, k, piece)
        return remote(ref, ref, ring_s, ring_r.at[flow, k, piece], right if flow == 0 else left)

    def ring_wait(flow, k, piece):
        ref, _ = ring(flow, k, piece)
        remote(ref, ref, ring_s, ring_r.at[flow, k - 1, piece], right).wait_recv()

    def meta_send(flow, k):
        _, at = ring(flow, k, 0)
        return remote(mt.at[at], mt.at[at], meta_s, meta_r.at[flow, k], right if flow == 0 else left)

    def meta_wait(flow, k):
        _, at = ring(flow, k, 0)
        remote(mt.at[at], mt.at[at], meta_s, meta_r.at[flow, k - 1], right).wait_recv()

    def picks(p):
        code = cw[p]
        own = jnp.where(code[0:1] == row16, 1.0, 0.0)
        other = jnp.where(code[1:2] == row16, 1.0, 0.0)
        return code, own, other

    def choose(k, at_a, at_b):
        p = k - 1
        ma, mb = mt[at_a], mt[at_b]
        named = jnp.where(lane < 64, ma, pltpu.roll(mb, 64, 1))
        weight = jnp.where(lane < 64, pltpu.roll(ma, 64, 1), mb)
        hit_own, hit_other = named == ex_own, named == ex_other
        has_own = jnp.sum(jnp.where(hit_own, 1.0, 0.0), axis=0, keepdims=True)
        has_other = jnp.sum(jnp.where(hit_other, 1.0, 0.0), axis=0, keepdims=True)
        w_own = jnp.sum(jnp.where(hit_own, weight, 0.0), axis=0, keepdims=True)
        w_other = jnp.sum(jnp.where(hit_other, weight, 0.0), axis=0, keepdims=True)
        has = jnp.where(sub == 0, has_own, jnp.where(sub == 1, has_other, 0.0))
        rank = jnp.dot(has.astype(BF16), tri[...], preferred_element_type=F32)
        rank = jnp.where(lane < 64, rank, rank + 8.0)
        code = jnp.where(has > 0.5, rank, -100.0)
        cw[p] = jnp.where(sub < 2, code, jnp.where(sub == 2, w_own, w_other))
        own = jnp.where(code[0:1] == row16, 1.0, 0.0)
        other = jnp.where(code[1:2] == row16, 1.0, 0.0)
        pick = jnp.concatenate([own, other], axis=0).astype(BF16)
        both = jnp.concatenate([blk[at_a], blk[at_b]], axis=0)
        rows = jnp.dot(pick, both, preferred_element_type=F32).astype(BF16)
        xg[dp, p, 0:16, :] = rows[0:16]
        ys[p] = rows[16:32]
        remote(ys.at[p], xg.at[dp, p, 16:32], y_s, y_r.at[p], ynb).start()

    def spread(p):
        remote(ys.at[p], xg.at[dp, p, 16:32], y_s, y_r.at[p], ynb).wait_recv()
        here = xg.at[dp, p]
        remote(here, here, x_s, x_r.at[0, p], x_up).start()
        remote(here, here, x_s, x_r.at[1, p], x_down).start()
        remote(here, here, pc_s, pc_r.at[0, p], core).start()

    def relay(p):
        low, high = xg.at[dp_down, p], xg.at[dp_up, p]
        remote(low, low, x_s, x_r.at[0, p], x_up).wait_recv()
        first = xg.at[dp_down, p, 0:16]
        remote(first, first, rel_s, rel_r.at[0, p], x_up).start()
        remote(low, low, pc_s, pc_r.at[1, p], core).start()
        remote(high, high, x_s, x_r.at[1, p], x_up).wait_recv()
        second = xg.at[dp_up, p, 16:32]
        remote(second, second, rel_s, rel_r.at[1, p], x_down).start()
        remote(high, high, pc_s, pc_r.at[2, p], core).start()

    def hand_over(p):
        first, second = xg.at[dp_far, p, 0:16], xg.at[dp_far, p, 16:32]
        remote(first, first, rel_s, rel_r.at[0, p], x_up).wait_recv()
        remote(second, second, rel_s, rel_r.at[1, p], x_up).wait_recv()
        far = xg.at[dp_far, p]
        remote(far, far, pc_s, pc_r.at[3, p], core).start()

    def gathered(p):
        here = xg.at[dp, p]
        for i in range(4):
            remote(here, here, pc_s, pc_r.at[i, p], core).wait_recv()

    for piece in range(CHUNKS):
        ring_send(0, 0, piece).start()
        ring_send(1, 0, piece).start()
    meta_send(0, 0).start()
    meta_send(1, 0).start()

    def ring_step(k, more_a, take_b, more_b):
        for piece in range(CHUNKS):
            ring_wait(0, k, piece)
            if more_a:
                ring_send(0, k, piece).start()
            if take_b:
                ring_wait(1, k, piece)
            if more_b:
                ring_send(1, k, piece).start()
        meta_wait(0, k)
        if more_a:
            meta_send(0, k).start()
        if take_b:
            meta_wait(1, k)
        if more_b:
            meta_send(1, k).start()
        at_a = lax.rem(z + n_z - k, n_z)
        at_b = lax.rem(z + k, n_z) if take_b else z
        choose(k, at_a, at_b)

    def body(k, carry):
        ring_step(k, True, True, True)
        pl.when(k >= 2)(lambda: spread(k - 2))
        pl.when(k >= 3)(lambda: relay(k - 3))
        pl.when(k >= 4)(lambda: hand_over(k - 4))
        return carry

    lax.fori_loop(1, half - 1, body, 0)
    ring_step(half - 1, True, True, False)
    spread(half - 3)
    relay(half - 4)
    hand_over(half - 5)
    ring_step(half, False, False, False)
    spread(half - 2)
    relay(half - 3)
    hand_over(half - 4)
    spread(half - 1)
    relay(half - 2)
    hand_over(half - 3)
    relay(half - 1)
    hand_over(half - 2)
    hand_over(half - 1)
    lax.fori_loop(0, half, lambda p, c: (gathered(p), c)[1], 0)

    load_gu.wait()
    load_dn.wait()
    span = half // GROUPS
    rows = span * 32
    hidden = guv.shape[1]
    contract = (((1,), (1,)), ((), ()))

    def group_at(g):
        return (GROUPS - 1 - g) * span

    def expand(g):
        p0 = group_at(g)
        gate = up = None
        for d in range(n_dp):
            part_x = xg[d, p0:p0 + span].reshape(rows, width)
            cols = slice(d * width, (d + 1) * width)
            a = lax.dot_general(part_x, guv[0, :, cols], contract, preferred_element_type=F32)
            b = lax.dot_general(part_x, guv[1, :, cols], contract, preferred_element_type=F32)
            gate, up = (a, b) if gate is None else (gate + a, up + b)
        ab[dp, p0 * 32:p0 * 32 + rows, :] = (gate / (1.0 + jnp.exp(-gate)) * up).astype(BF16)
        here = ab.at[dp, p0 * 32:p0 * 32 + rows]
        remote(here, here, ax_s, ax_r.at[0, g], x_up).start()
        remote(here, here, ax_s, ax_r.at[1, g], x_down).start()
        remote(here, here, ap_s, ap_r.at[0, g], core).start()

    def act_relay(g):
        r0 = group_at(g) * 32
        mid, end = r0 + rows // 2, r0 + rows
        low, high = ab.at[dp_down, r0:end], ab.at[dp_up, r0:end]
        remote(low, low, ax_s, ax_r.at[0, g], x_up).wait_recv()
        first = ab.at[dp_down, r0:mid]
        remote(first, first, al_s, al_r.at[0, g], x_up).start()
        remote(low, low, ap_s, ap_r.at[1, g], core).start()
        remote(high, high, ax_s, ax_r.at[1, g], x_up).wait_recv()
        second = ab.at[dp_up, mid:end]
        remote(second, second, al_s, al_r.at[1, g], x_down).start()
        remote(high, high, ap_s, ap_r.at[2, g], core).start()

    def act_hand_over(g):
        r0 = group_at(g) * 32
        mid, end = r0 + rows // 2, r0 + rows
        first, second = ab.at[dp_far, r0:mid], ab.at[dp_far, mid:end]
        remote(first, first, al_s, al_r.at[0, g], x_up).wait_recv()
        remote(second, second, al_s, al_r.at[1, g], x_up).wait_recv()
        far = ab.at[dp_far, r0:end]
        remote(far, far, ap_s, ap_r.at[3, g], core).start()

    def contract_down(g):
        p0 = group_at(g)
        r0 = p0 * 32
        here = ab.at[dp, r0:r0 + rows]
        for i in range(4):
            remote(here, here, ap_s, ap_r.at[i, g], core).wait_recv()
        total = None
        for d in range(n_dp):
            a = jnp.dot(
                ab[d, r0:r0 + rows, :], dnv[d * hidden:(d + 1) * hidden, :], preferred_element_type=F32
            )
            total = a if total is None else total + a
        eo[p0:p0 + span] = total.astype(BF16).reshape(span, 32, width)
        rr[p0:p0 + span, 0:16, :] = eo[p0:p0 + span, 0:16, :]
        remote(
            eo.at[p0:p0 + span, 16:32], rr.at[p0:p0 + span, 16:32], yb_s, yb_r.at[g], ynb
        ).start()

    def swapped(g):
        p0 = group_at(g)
        there = rr.at[p0:p0 + span, 16:32]
        remote(there, there, yb_s, yb_r.at[g], ynb).wait_recv()

    expand(0)
    expand(1)
    act_relay(0)
    expand(2)
    act_hand_over(0)
    act_relay(1)
    contract_down(0)
    expand(3)
    act_hand_over(1)
    act_relay(2)
    contract_down(1)
    act_hand_over(2)
    act_relay(3)
    contract_down(2)
    act_hand_over(3)
    contract_down(3)
    for g in range(GROUPS):
        swapped(g)

    def share(k):
        code, own, other = picks(k - 1)
        w = jnp.concatenate([own * code[2:3], other * code[3:4]], axis=0)
        w_high = w.astype(BF16)
        w_low = (w - w_high.astype(F32)).astype(BF16)
        lhs = jnp.concatenate([w_high, w_low], axis=0)
        res = rr[k - 1]
        rhs = jnp.concatenate([res, res], axis=0)
        return lax.dot_general(lhs, rhs, (((0,), (0,)), ((), ())), preferred_element_type=F32)

    def back_send(flow, k, piece):
        buf = rbl if flow == 0 else rbr
        cut = pl.ds(piece * part, part)
        return remote(
            buf.at[k, cut], buf.at[k - 1, cut], rs_s, rs_r.at[flow, k - 1, piece], left if flow == 0 else right
        )

    def back_wait(flow, k, piece):
        buf = rbl if flow == 0 else rbr
        ref = buf.at[k, pl.ds(piece * part, part)]
        remote(ref, ref, rs_s, rs_r.at[flow, k, piece], left).wait_recv()

    def back_step(k, start_a, start_b):
        for piece in range(CHUNKS):
            lo = piece * part
            if not start_a:
                back_wait(0, k, piece)
            add = ct[lo:lo + part, :]
            if not start_a:
                add = add + rbl[k, lo:lo + part, :].astype(F32)
            rbl[k, lo:lo + part, :] = add.astype(BF16)
            back_send(0, k, piece).start()
            if start_b is None:
                continue
            if not start_b:
                back_wait(1, k, piece)
            add = ct[tokens + lo:tokens + lo + part, :]
            if not start_b:
                add = add + rbr[k, lo:lo + part, :].astype(F32)
            rbr[k, lo:lo + part, :] = add.astype(BF16)
            back_send(1, k, piece).start()

    ct[...] = share(half)
    oc[...] = ct[tokens:, :] + x_ref[:, mine].astype(F32)
    back_step(half, True, None)
    ct[...] = share(half - 1)
    back_step(half - 1, False, True)

    def back_body(i, carry):
        k = half - 2 - i
        ct[...] = share(k)
        back_step(k, False, False)
        return carry

    lax.fori_loop(0, half - 2, back_body, 0)
    for piece in range(CHUNKS):
        lo = piece * part
        back_wait(0, 0, piece)
        back_wait(1, 0, piece)
        fin[lo:lo + part, :] = (
            oc[lo:lo + part, :] + rbl[0, lo:lo + part, :].astype(F32) + rbr[0, lo:lo + part, :].astype(F32)
        ).astype(BF16)
    last = remote(fin, out_ref, fin_s, fin_r, over)
    last.start()

    def drained(ref, sem):
        remote(ref, ref, sem, sem, right).wait_send()

    drained(blk.at[0:n_z - 1], ring_s)
    drained(mt.at[0:n_z - 1], meta_s)
    drained(ys, y_s)
    drained(xg.at[0:2], x_s)
    drained(xg.at[0], rel_s)
    drained(xg.at[0:4], pc_s)
    drained(ab.at[0:2], ax_s)
    drained(ab.at[0], al_s)
    drained(ab.at[0:4], ap_s)
    drained(ys, yb_s)
    drained(blk.at[0:n_z - 1], rs_s)
    last.wait()


def body(activations, routes, gate_weights, norm_gain, gate_up_weights, down_weights):
    n_dp, n_exp = lax.axis_size("dp"), lax.axis_size("expert")
    tokens, features = activations.shape[1:]
    hidden = gate_up_weights.shape[2]
    width = features // n_dp
    n_z = n_exp // 2
    half = n_z // 2
    named = jnp.concatenate([routes[0].T.astype(F32), gate_weights[0].T], axis=1)
    vmem, anywhere = pl.BlockSpec(memory_space=pltpu.VMEM), pl.BlockSpec(memory_space=pl.ANY)
    dma = pltpu.SemaphoreType.DMA
    out = pl.pallas_call(
        functools.partial(kernel, n_dp, n_exp),
        out_shape=jax.ShapeDtypeStruct((tokens, width), BF16),
        in_specs=[vmem, vmem, vmem, anywhere, anywhere],
        out_specs=vmem,
        scratch_shapes=[
            pltpu.VMEM((2, hidden, features), BF16),
            pltpu.VMEM((hidden * n_dp, width), BF16),
            pltpu.VMEM((n_z, tokens, width), BF16),
            pltpu.VMEM((n_z, 8, 128), F32),
            pltpu.VMEM((half, 8, 128), F32),
            pltpu.VMEM((128, 128), BF16),
            pltpu.VMEM((half, 16, width), BF16),
            pltpu.VMEM((n_dp, half, 32, width), BF16),
            pltpu.VMEM((n_dp, half * 32, hidden), BF16),
            pltpu.VMEM((half, 32, width), BF16),
            pltpu.VMEM((half, 32, width), BF16),
            pltpu.VMEM((half + 1, tokens, width), BF16),
            pltpu.VMEM((half, tokens, width), BF16),
            pltpu.VMEM((2 * tokens, width), F32),
            pltpu.VMEM((tokens, width), F32),
            pltpu.VMEM((tokens, width), BF16),
            dma((2,)),
            dma, dma((2, half, CHUNKS)),
            dma, dma((2, half)),
            dma, dma((half,)),
            dma, dma((2, half)),
            dma, dma((2, half)),
            dma, dma((4, half)),
            dma, dma((2, GROUPS)),
            dma, dma((2, GROUPS)),
            dma, dma((4, GROUPS)),
            dma, dma((GROUPS,)),
            dma, dma((2, half, CHUNKS)),
            dma, dma,
        ],
        compiler_params=pltpu.CompilerParams(
            collective_id=0, has_side_effects=True, vmem_limit_bytes=56 * 1024 * 1024
        ),
    )(activations[0], named, norm_gain[None], gate_up_weights[0], down_weights[0])
    return out[None]


def solution(mesh):
    placed = (
        P("section", "expert", None),
        P("section", "expert", None),
        P("section", "expert", None),
        P(),
        P("expert", None, "dp", None),
        P("expert", None, "dp"),
    )
    return jax.shard_map(
        body, mesh=mesh, in_specs=placed, out_specs=P("section", "expert", "dp"), check_vma=False
    )
```

```python
import functools

import jax
import jax.numpy as jnp
from jax import lax
from jax.experimental import pallas as pl
from jax.experimental.pallas import tpu as pltpu
from jax.sharding import PartitionSpec as P

MESH = pl.DeviceIdType.MESH
F32, BF16 = jnp.float32, jnp.bfloat16
CHUNKS = 2
GROUPS = 4


def remote(src, dst, send, recv, device):
    return pltpu.make_async_remote_copy(
        src_ref=src, dst_ref=dst, send_sem=send, recv_sem=recv, device_id=device, device_id_type=MESH
    )


def kernel(
    n_dp, n_exp,
    x_ref, routes_ref, gates_ref, gain_ref, gu_hbm, dn_hbm, out_ref,
    guv, dnv, blk, mt, cw, tri, ys, xg, ab, eo, rr, rbl, rbr, ct, oc, fin, lfl, lfr,
    load_sem, ring_s, ring_r, meta_s, meta_r, y_s, y_r, x_s, x_r, rel_s, rel_r, pc_s, pc_r,
    ax_s, ax_r, al_s, al_r, ap_s, ap_r, yb_s, yb_r, rs_s, rs_r, lf_s, lf_r, fin_s, fin_r,
):
    sec, dp, ex = lax.axis_index("section"), lax.axis_index("dp"), lax.axis_index("expert")
    n_z = n_exp // 2
    half = n_z // 2
    z, yl = ex // 2, lax.rem(ex, 2)
    tokens, width = blk.shape[1], blk.shape[2]
    part = tokens // CHUNKS
    right = (sec, dp, lax.rem(ex + 2, n_exp))
    left = (sec, dp, lax.rem(ex + n_exp - 2, n_exp))
    right2 = (sec, dp, lax.rem(ex + 4, n_exp))
    left2 = (sec, dp, lax.rem(ex + n_exp - 4, n_exp))
    ynb = (sec, dp, ex + 1 - 2 * yl)
    dp_up, dp_down = lax.rem(dp + 2, n_dp), lax.rem(dp + n_dp - 2, n_dp)
    dp_far = lax.rem(dp + n_dp // 2, n_dp)
    dp_pc = dp + 1 - 2 * lax.rem(dp, 2)
    x_up, x_down, core = (sec, dp_up, ex), (sec, dp_down, ex), (sec, dp_pc, ex)
    over = (1 - sec, dp, ex)

    barrier = pltpu.get_barrier_semaphore()
    for peer in (right, left, right2, left2, ynb, x_up, x_down, core, over):
        pl.semaphore_signal(barrier, inc=1, device_id=peer, device_id_type=MESH)
    load_gu = pltpu.make_async_copy(gu_hbm, guv, load_sem.at[0])
    load_dn = pltpu.make_async_copy(dn_hbm, dnv, load_sem.at[1])
    load_gu.start()
    load_dn.start()

    wide = x_ref[...].astype(F32)
    scale = lax.rsqrt(jnp.mean(wide * wide, axis=-1, keepdims=True) + 1e-06)
    mine = pl.ds(pl.multiple_of(dp * width, width), width)
    blk[z] = (x_ref[:, mine].astype(F32) * scale * gain_ref[:, mine].astype(F32)).astype(BF16)
    mt[z, :, 0:64] = routes_ref[...].astype(F32)
    mt[z, :, 64:128] = gates_ref[...]
    a_tok = lax.broadcasted_iota(jnp.int32, (128, 128), 0)
    b_tok = lax.broadcasted_iota(jnp.int32, (128, 128), 1)
    tri[...] = jnp.where((a_tok < b_tok) & ((a_tok < 64) == (b_tok < 64)), 1.0, 0.0).astype(BF16)
    lane = lax.broadcasted_iota(jnp.int32, (8, 128), 1)
    sub = lax.broadcasted_iota(jnp.int32, (8, 128), 0)
    row16 = lax.broadcasted_iota(jnp.int32, (16, 128), 0).astype(F32)
    ex_own, ex_other = ex.astype(F32), (ex + 1 - 2 * yl).astype(F32)
    pl.semaphore_wait(barrier, 9)

    def place(flow, k):
        return lax.rem(z + n_z - k, n_z) if flow == 0 else lax.rem(z + k, n_z)

    def target(flow, hops):
        return ((right, right2) if flow == 0 else (left, left2))[hops - 1]

    def ring_send(flow, k, hops, piece):
        ref = blk.at[place(flow, k), pl.ds(piece * part, part)]
        remote(ref, ref, ring_s, ring_r.at[flow, k + hops - 1, piece], target(flow, hops)).start()

    def ring_wait(flow, k, piece):
        ref = blk.at[place(flow, k), pl.ds(piece * part, part)]
        remote(ref, ref, ring_s, ring_r.at[flow, k - 1, piece], right).wait_recv()

    def meta_send(flow, k, hops):
        ref = mt.at[place(flow, k)]
        remote(ref, ref, meta_s, meta_r.at[flow, k + hops - 1], target(flow, hops)).start()

    def meta_wait(flow, k):
        ref = mt.at[place(flow, k)]
        remote(ref, ref, meta_s, meta_r.at[flow, k - 1], right).wait_recv()

    def picks(p):
        code = cw[p]
        own = jnp.where(code[0:1] == row16, 1.0, 0.0)
        other = jnp.where(code[1:2] == row16, 1.0, 0.0)
        return code, own, other

    def choose(k, at_a, at_b):
        p = k - 1
        ma, mb = mt[at_a], mt[at_b]
        named = jnp.where(lane < 64, ma, pltpu.roll(mb, 64, 1))
        weight = jnp.where(lane < 64, pltpu.roll(ma, 64, 1), mb)
        hit_own, hit_other = named == ex_own, named == ex_other
        has_own = jnp.sum(jnp.where(hit_own, 1.0, 0.0), axis=0, keepdims=True)
        has_other = jnp.sum(jnp.where(hit_other, 1.0, 0.0), axis=0, keepdims=True)
        w_own = jnp.sum(jnp.where(hit_own, weight, 0.0), axis=0, keepdims=True)
        w_other = jnp.sum(jnp.where(hit_other, weight, 0.0), axis=0, keepdims=True)
        has = jnp.where(sub == 0, has_own, jnp.where(sub == 1, has_other, 0.0))
        rank = jnp.dot(has.astype(BF16), tri[...], preferred_element_type=F32)
        rank = jnp.where(lane < 64, rank, rank + 8.0)
        code = jnp.where(has > 0.5, rank, -100.0)
        cw[p] = jnp.where(sub < 2, code, jnp.where(sub == 2, w_own, w_other))
        own = jnp.where(code[0:1] == row16, 1.0, 0.0)
        other = jnp.where(code[1:2] == row16, 1.0, 0.0)
        pick = jnp.concatenate([own, other], axis=0).astype(BF16)
        both = jnp.concatenate([blk[at_a], blk[at_b]], axis=0)
        rows = jnp.dot(pick, both, preferred_element_type=F32).astype(BF16)
        xg[dp, p, 0:16, :] = rows[0:16]
        ys[p] = rows[16:32]

    def swap(m):
        return remote(ys.at[pl.ds(2 * m, 2)], xg.at[dp, pl.ds(2 * m, 2), 16:32], y_s, y_r.at[m], ynb)

    def rows_of(d, m):
        return xg.at[d, pl.ds(2 * m, 2)]

    def spread(m):
        swap(m).wait_recv()
        here = rows_of(dp, m)
        remote(here, here, x_s, x_r.at[0, m], x_up).start()
        remote(here, here, x_s, x_r.at[1, m], x_down).start()
        remote(here, here, pc_s, pc_r.at[0, m], core).start()

    def relay(m):
        low, high = rows_of(dp_down, m), rows_of(dp_up, m)
        remote(low, low, x_s, x_r.at[0, m], x_up).wait_recv()
        first = xg.at[dp_down, 2 * m]
        remote(first, first, rel_s, rel_r.at[0, m], x_up).start()
        remote(high, high, x_s, x_r.at[1, m], x_up).wait_recv()
        second = xg.at[dp_up, 2 * m + 1]
        remote(second, second, rel_s, rel_r.at[1, m], x_down).start()
        remote(low, low, pc_s, pc_r.at[1, m], core).start()
        remote(high, high, pc_s, pc_r.at[2, m], core).start()

    def hand_over(m):
        first, second = xg.at[dp_far, 2 * m], xg.at[dp_far, 2 * m + 1]
        remote(first, first, rel_s, rel_r.at[0, m], x_up).wait_recv()
        remote(second, second, rel_s, rel_r.at[1, m], x_up).wait_recv()
        far = rows_of(dp_far, m)
        remote(far, far, pc_s, pc_r.at[3, m], core).start()

    def gathered(m):
        here = rows_of(dp, m)
        for i in range(4):
            remote(here, here, pc_s, pc_r.at[i, m], core).wait_recv()

    for piece in range(CHUNKS):
        for hops in (2, 1):
            for flow in (0, 1):
                ring_send(flow, 0, hops, piece)
    for hops in (2, 1):
        for flow in (0, 1):
            meta_send(flow, 0, hops)

    def ring_step(m, evens, sends):
        k = 2 * m
        for piece in range(CHUNKS):
            for flow in evens:
                ring_wait(flow, k, piece)
                for hops in sends[flow]:
                    ring_send(flow, k, hops, piece)
        for flow in evens:
            meta_wait(flow, k)
            for hops in sends[flow]:
                meta_send(flow, k, hops)
        for flow in (0, 1):
            for piece in range(CHUNKS):
                ring_wait(flow, k - 1, piece)
            meta_wait(flow, k - 1)
        choose(k - 1, place(0, k - 1), place(1, k - 1))
        choose(k, place(0, k), place(1, k) if 1 in evens else z)
        swap(m - 1).start()

    def body(m, carry):
        ring_step(m, (0, 1), ((2, 1), (2, 1)))
        pl.when(m >= 2)(lambda: spread(m - 2))
        pl.when(m >= 3)(lambda: relay(m - 3))
        pl.when(m >= 4)(lambda: hand_over(m - 4))
        return carry

    sets = half // 2
    lax.fori_loop(1, sets - 1, body, 0)
    ring_step(sets - 1, (0, 1), ((2, 1), (1,)))
    spread(sets - 3)
    relay(sets - 4)
    hand_over(sets - 5)
    ring_step(sets, (0,), ((), ()))
    spread(sets - 2)
    relay(sets - 3)
    hand_over(sets - 4)
    spread(sets - 1)
    relay(sets - 2)
    hand_over(sets - 3)
    relay(sets - 1)
    hand_over(sets - 2)
    hand_over(sets - 1)
    lax.fori_loop(0, sets, lambda m, c: (gathered(m), c)[1], 0)

    load_gu.wait()
    load_dn.wait()
    span = half // GROUPS
    rows = span * 32
    hidden = guv.shape[1]
    contract = (((1,), (1,)), ((), ()))

    def group_at(g):
        return (GROUPS - 1 - g) * span

    def expand(g):
        p0 = group_at(g)
        gate = up = None
        for d in range(n_dp):
            part_x = xg[d, p0:p0 + span].reshape(rows, width)
            cols = slice(d * width, (d + 1) * width)
            a = lax.dot_general(part_x, guv[0, :, cols], contract, preferred_element_type=F32)
            b = lax.dot_general(part_x, guv[1, :, cols], contract, preferred_element_type=F32)
            gate, up = (a, b) if gate is None else (gate + a, up + b)
        ab[dp, p0 * 32:p0 * 32 + rows, :] = (gate / (1.0 + jnp.exp(-gate)) * up).astype(BF16)
        here = ab.at[dp, p0 * 32:p0 * 32 + rows]
        remote(here, here, ax_s, ax_r.at[0, g], x_up).start()
        remote(here, here, ax_s, ax_r.at[1, g], x_down).start()
        remote(here, here, ap_s, ap_r.at[0, g], core).start()

    def act_relay(g):
        r0 = group_at(g) * 32
        mid, end = r0 + rows // 2, r0 + rows
        low, high = ab.at[dp_down, r0:end], ab.at[dp_up, r0:end]
        remote(low, low, ax_s, ax_r.at[0, g], x_up).wait_recv()
        first = ab.at[dp_down, r0:mid]
        remote(first, first, al_s, al_r.at[0, g], x_up).start()
        remote(low, low, ap_s, ap_r.at[1, g], core).start()
        remote(high, high, ax_s, ax_r.at[1, g], x_up).wait_recv()
        second = ab.at[dp_up, mid:end]
        remote(second, second, al_s, al_r.at[1, g], x_down).start()
        remote(high, high, ap_s, ap_r.at[2, g], core).start()

    def act_hand_over(g):
        r0 = group_at(g) * 32
        mid, end = r0 + rows // 2, r0 + rows
        first, second = ab.at[dp_far, r0:mid], ab.at[dp_far, mid:end]
        remote(first, first, al_s, al_r.at[0, g], x_up).wait_recv()
        remote(second, second, al_s, al_r.at[1, g], x_up).wait_recv()
        far = ab.at[dp_far, r0:end]
        remote(far, far, ap_s, ap_r.at[3, g], core).start()

    def contract_down(g):
        p0 = group_at(g)
        r0 = p0 * 32
        here = ab.at[dp, r0:r0 + rows]
        for i in range(4):
            remote(here, here, ap_s, ap_r.at[i, g], core).wait_recv()
        total = None
        for d in range(n_dp):
            a = jnp.dot(
                ab[d, r0:r0 + rows, :], dnv[d * hidden:(d + 1) * hidden, :], preferred_element_type=F32
            )
            total = a if total is None else total + a
        eo[p0:p0 + span] = total.astype(BF16).reshape(span, 32, width)
        rr[p0:p0 + span, 0:16, :] = eo[p0:p0 + span, 0:16, :]
        remote(
            eo.at[p0:p0 + span, 16:32], rr.at[p0:p0 + span, 16:32], yb_s, yb_r.at[g], ynb
        ).start()

    def swapped(g):
        p0 = group_at(g)
        there = rr.at[p0:p0 + span, 16:32]
        remote(there, there, yb_s, yb_r.at[g], ynb).wait_recv()

    def share(k):
        code, own, other = picks(k - 1)
        w = jnp.concatenate([own * code[2:3], other * code[3:4]], axis=0)
        w_high = w.astype(BF16)
        w_low = (w - w_high.astype(F32)).astype(BF16)
        lhs = jnp.concatenate([w_high, w_low], axis=0)
        res = rr[k - 1]
        rhs = jnp.concatenate([res, res], axis=0)
        return lax.dot_general(lhs, rhs, (((0,), (0,)), ((), ())), preferred_element_type=F32)

    def leaf_send(flow, k):
        buf = (lfl, lfr)[flow]
        half_ct = slice(0, tokens) if flow == 0 else slice(tokens, 2 * tokens)
        buf[k] = ct[1, half_ct, :].astype(BF16)
        remote(buf.at[k], buf.at[k - 1], lf_s, lf_r.at[flow, k - 1], target(1 - flow, 1)).start()

    def leaf_wait(flow, k):
        ref = (lfl, lfr)[flow].at[k]
        remote(ref, ref, lf_s, lf_r.at[flow, k], left).wait_recv()

    def back_wait(flow, k, piece):
        ref = (rbl, rbr)[flow].at[k, pl.ds(piece * part, part)]
        remote(ref, ref, rs_s, rs_r.at[flow, k, piece], left).wait_recv()

    def chain(flow, k, piece, leaf, more):
        buf, leaves = (rbl, rbr)[flow], (lfl, lfr)[flow]
        cut = slice(piece * part, (piece + 1) * part)
        add = ct[0, flow * tokens + piece * part:flow * tokens + (piece + 1) * part, :]
        if leaf:
            add = add + leaves[k, cut, :].astype(F32)
        if more:
            back_wait(flow, k, piece)
            add = add + buf[k, cut, :].astype(F32)
        buf[k, cut, :] = add.astype(BF16)
        remote(
            buf.at[k, cut], buf.at[k - 2, cut], rs_s, rs_r.at[flow, k - 2, piece], target(1 - flow, 2)
        ).start()

    def shares_for(m):
        ct[0] = share(2 * m)
        ct[1] = share(2 * m - 1)

    def back_step(m):
        k = 2 * m
        if k < half:
            leaf_wait(0, k)
            leaf_wait(1, k)
        for piece in range(CHUNKS):
            chain(0, k, piece, k < half, k < half)
            if k < half:
                chain(1, k, piece, True, k < half - 2)
        leaf_send(0, k - 1)
        leaf_send(1, k - 1)

    def back_pair(g):
        m = (GROUPS - g) * span // 2
        swapped(g)
        shares_for(m)
        if g == 0:
            oc[...] = ct[0, tokens:, :] + x_ref[:, mine].astype(F32)
        back_step(m)
        shares_for(m - 1)
        return m - 1

    expand(0)
    expand(1)
    act_relay(0)
    expand(2)
    act_hand_over(0)
    act_relay(1)
    contract_down(0)
    expand(3)
    act_hand_over(1)
    m = back_pair(0)
    act_relay(2)
    contract_down(1)
    back_step(m)
    m = back_pair(1)
    act_hand_over(2)
    act_relay(3)
    contract_down(2)
    back_step(m)
    m = back_pair(2)
    act_hand_over(3)
    contract_down(3)
    back_step(m)
    m = back_pair(3)
    back_step(m)
    leaf_wait(0, 0)
    leaf_wait(1, 0)
    for piece in range(CHUNKS):
        cut = slice(piece * part, (piece + 1) * part)
        near = oc[cut, :] + lfl[0, cut, :].astype(F32) + lfr[0, cut, :].astype(F32)
        back_wait(0, 0, piece)
        back_wait(1, 0, piece)
        fin[cut, :] = (near + rbl[0, cut, :].astype(F32) + rbr[0, cut, :].astype(F32)).astype(BF16)
    last = remote(fin, out_ref, fin_s, fin_r, over)
    last.start()

    def drained(ref, sem):
        remote(ref, ref, sem, sem, right).wait_send()

    drained(blk.at[0:n_z - 1], ring_s)
    drained(mt.at[0:n_z - 1], meta_s)
    drained(ys, y_s)
    drained(xg.at[0:2], x_s)
    drained(xg.at[0], rel_s)
    drained(xg.at[0:4], pc_s)
    drained(ab.at[0:2], ax_s)
    drained(ab.at[0], al_s)
    drained(ab.at[0:4], ap_s)
    drained(ys, yb_s)
    drained(blk.at[0:half - 1], rs_s)
    drained(blk.at[0:half], lf_s)
    last.wait()


def body(activations, routes, gate_weights, norm_gain, gate_up_weights, down_weights):
    n_dp, n_exp = lax.axis_size("dp"), lax.axis_size("expert")
    tokens, features = activations.shape[1:]
    hidden = gate_up_weights.shape[2]
    width = features // n_dp
    n_z = n_exp // 2
    half = n_z // 2
    vmem, anywhere = pl.BlockSpec(memory_space=pltpu.VMEM), pl.BlockSpec(memory_space=pl.ANY)
    dma = pltpu.SemaphoreType.DMA
    out = pl.pallas_call(
        functools.partial(kernel, n_dp, n_exp),
        out_shape=jax.ShapeDtypeStruct((tokens, width), BF16),
        in_specs=[vmem, vmem, vmem, vmem, anywhere, anywhere],
        out_specs=vmem,
        scratch_shapes=[
            pltpu.VMEM((2, hidden, features), BF16),
            pltpu.VMEM((hidden * n_dp, width), BF16),
            pltpu.VMEM((n_z, tokens, width), BF16),
            pltpu.VMEM((n_z, 8, 128), F32),
            pltpu.VMEM((half, 8, 128), F32),
            pltpu.VMEM((128, 128), BF16),
            pltpu.VMEM((half, 16, width), BF16),
            pltpu.VMEM((n_dp, half, 32, width), BF16),
            pltpu.VMEM((n_dp, half * 32, hidden), BF16),
            pltpu.VMEM((half, 32, width), BF16),
            pltpu.VMEM((half, 32, width), BF16),
            pltpu.VMEM((half + 1, tokens, width), BF16),
            pltpu.VMEM((half, tokens, width), BF16),
            pltpu.VMEM((2, 2 * tokens, width), F32),
            pltpu.VMEM((tokens, width), F32),
            pltpu.VMEM((tokens, width), BF16),
            pltpu.VMEM((half, tokens, width), BF16),
            pltpu.VMEM((half, tokens, width), BF16),
            dma((2,)),
            dma, dma((2, half, CHUNKS)),
            dma, dma((2, half)),
            dma, dma((half // 2,)),
            dma, dma((2, half // 2)),
            dma, dma((2, half // 2)),
            dma, dma((4, half // 2)),
            dma, dma((2, GROUPS)),
            dma, dma((2, GROUPS)),
            dma, dma((4, GROUPS)),
            dma, dma((GROUPS,)),
            dma, dma((2, half, CHUNKS)),
            dma, dma((2, half)),
            dma, dma,
        ],
        compiler_params=pltpu.CompilerParams(
            collective_id=0, has_side_effects=True, vmem_limit_bytes=56 * 1024 * 1024
        ),
    )(activations[0], routes[0].T, gate_weights[0].T, norm_gain[None], gate_up_weights[0], down_weights[0])
    return out[None]


def solution(mesh):
    placed = (
        P("section", "expert", None),
        P("section", "expert", None),
        P("section", "expert", None),
        P(),
        P("expert", None, "dp", None),
        P("expert", None, "dp"),
    )
    return jax.shard_map(
        body, mesh=mesh, in_specs=placed, out_specs=P("section", "expert", "dp"), check_vma=False
    )
```

```python
import functools

import jax
import jax.numpy as jnp
from jax import lax
from jax.experimental import pallas as pl
from jax.experimental.pallas import tpu as pltpu
from jax.sharding import PartitionSpec as P

MESH = pl.DeviceIdType.MESH
F32, BF16 = jnp.float32, jnp.bfloat16
CHUNKS = 2
GROUPS = 4


def remote(src, dst, send, recv, device):
    return pltpu.make_async_remote_copy(
        src_ref=src, dst_ref=dst, send_sem=send, recv_sem=recv, device_id=device, device_id_type=MESH
    )


def kernel(
    n_dp, n_exp,
    x_ref, routes_ref, gates_ref, gain_ref, gu_hbm, dn_hbm, out_ref,
    guv, dnv, blk, mt, cw, tri, ys, xg, ab, eo, rr, rbl, rbr, ct, oc, fin, lin, lout, bin_, bout,
    load_sem, ring_s, ring_r, meta_s, meta_r, leaf_s, leaf_r, y_s, y_r, x_s, x_r, rel_s, rel_r, pc_s, pc_r,
    ax_s, ax_r, al_s, al_r, ap_s, ap_r, yb_s, yb_r, rs_s, rs_r, lf_s, lf_r, fin_s, fin_r,
):
    sec, dp, ex = lax.axis_index("section"), lax.axis_index("dp"), lax.axis_index("expert")
    n_z = n_exp // 2
    half = n_z // 2
    z, yl = ex // 2, lax.rem(ex, 2)
    tokens, width = blk.shape[1], blk.shape[2]
    part = tokens // CHUNKS
    right = (sec, dp, lax.rem(ex + 2, n_exp))
    left = (sec, dp, lax.rem(ex + n_exp - 2, n_exp))
    right2 = (sec, dp, lax.rem(ex + 4, n_exp))
    left2 = (sec, dp, lax.rem(ex + n_exp - 4, n_exp))
    ynb = (sec, dp, ex + 1 - 2 * yl)
    dp_up, dp_down = lax.rem(dp + 2, n_dp), lax.rem(dp + n_dp - 2, n_dp)
    dp_far = lax.rem(dp + n_dp // 2, n_dp)
    dp_pc = dp + 1 - 2 * lax.rem(dp, 2)
    x_up, x_down, core = (sec, dp_up, ex), (sec, dp_down, ex), (sec, dp_pc, ex)
    over = (1 - sec, dp, ex)

    barrier = pltpu.get_barrier_semaphore()
    for peer in (right, left, right2, left2, ynb, x_up, x_down, core, over):
        pl.semaphore_signal(barrier, inc=1, device_id=peer, device_id_type=MESH)
    load_gu = pltpu.make_async_copy(gu_hbm, guv, load_sem.at[0])
    load_dn = pltpu.make_async_copy(dn_hbm, dnv, load_sem.at[1])
    load_gu.start()
    load_dn.start()

    wide = x_ref[...].astype(F32)
    scale = lax.rsqrt(jnp.mean(wide * wide, axis=-1, keepdims=True) + 1e-06)
    mine = pl.ds(pl.multiple_of(dp * width, width), width)
    blk[z] = (x_ref[:, mine].astype(F32) * scale * gain_ref[:, mine].astype(F32)).astype(BF16)
    mt[z, :, 0:64] = routes_ref[...].astype(F32)
    mt[z, :, 64:128] = gates_ref[...]
    a_tok = lax.broadcasted_iota(jnp.int32, (128, 128), 0)
    b_tok = lax.broadcasted_iota(jnp.int32, (128, 128), 1)
    tri[...] = jnp.where((a_tok < b_tok) & ((a_tok < 64) == (b_tok < 64)), 1.0, 0.0).astype(BF16)
    lane = lax.broadcasted_iota(jnp.int32, (8, 128), 1)
    sub = lax.broadcasted_iota(jnp.int32, (8, 128), 0)
    row16 = lax.broadcasted_iota(jnp.int32, (16, 128), 0).astype(F32)
    low16 = lax.broadcasted_iota(jnp.int32, (16, 128), 1) < 64
    first16 = row16 < 8.0
    mate = 1 - 2 * yl
    ahead, behind = lax.rem(ex + 2, n_exp), lax.rem(ex + n_exp - 2, n_exp)
    wanted = (
        jnp.full((8, 128), ex, jnp.int32),
        jnp.full((8, 128), ex + mate, jnp.int32),
        jnp.where(lane < 64, ahead, behind),
        jnp.where(lane < 64, ahead + mate, behind + mate),
    )
    pl.semaphore_wait(barrier, 9)

    def place(flow, k):
        return lax.rem(z + n_z - k, n_z) if flow == 0 else lax.rem(z + k, n_z)

    def target(flow, hops):
        return ((right, right2) if flow == 0 else (left, left2))[hops - 1]

    def ring_send(flow, j, piece):
        ref = blk.at[place(flow, 2 * j), pl.ds(piece * part, part)]
        remote(ref, ref, ring_s, ring_r.at[flow, j, piece], target(flow, 2)).start()

    def ring_wait(flow, j, piece):
        ref = blk.at[place(flow, 2 * j), pl.ds(piece * part, part)]
        remote(ref, ref, ring_s, ring_r.at[flow, j - 1, piece], right).wait_recv()

    def meta_send(flow, j):
        ref = mt.at[place(flow, 2 * j)]
        remote(ref, ref, meta_s, meta_r.at[flow, j], target(flow, 2)).start()

    def meta_wait(flow, j):
        ref = mt.at[place(flow, 2 * j)]
        remote(ref, ref, meta_s, meta_r.at[flow, j - 1], right).wait_recv()

    def masks(code):
        own = jnp.where(code[0:1] == row16, 1.0, 0.0)
        other = jnp.where(code[1:2] == row16, 1.0, 0.0)
        at_a = jnp.where(first16, code[2:3], code[3:4] + 8.0)
        at_b = jnp.where(first16, code[2:3] - 8.0, code[3:4])
        leaf_a = jnp.where((at_a == row16) & low16, 1.0, 0.0)
        leaf_b = jnp.where((at_b == row16) & ~low16, 1.0, 0.0)
        return own, other, leaf_a, leaf_b

    def choose(j, at_a, at_b, own, leaf):
        ma, mb = mt[at_a], mt[at_b]
        named = jnp.where(lane < 64, ma, pltpu.roll(mb, 64, 1))
        weight = jnp.where(lane < 64, pltpu.roll(ma, 64, 1), mb)
        has = weights = jnp.zeros((8, 128), F32)
        for i, expert in enumerate(wanted):
            hit = named == expert.astype(F32)
            has = jnp.where(sub == i, jnp.sum(jnp.where(hit, 1.0, 0.0), axis=0, keepdims=True), has)
            weights = jnp.where(sub == 4 + i, jnp.sum(jnp.where(hit, weight, 0.0), axis=0, keepdims=True), weights)
        rank = jnp.dot(has.astype(BF16), tri[...], preferred_element_type=F32)
        rank = jnp.where(lane < 64, rank, rank + 8.0)
        code = jnp.where(sub < 4, jnp.where(has > 0.5, rank, -100.0), weights)
        cw[j] = code
        mask = masks(code)
        mask = (mask[:2] if own else ()) + (mask[2:] if leaf else ())
        pick = jnp.concatenate(mask, axis=0).astype(BF16)
        both = jnp.concatenate([blk[at_a], blk[at_b]], axis=0)
        rows = jnp.dot(pick, both, preferred_element_type=F32).astype(BF16)
        if leaf:
            lout[0, j] = rows[-32:-16]
            lout[1, j] = rows[-16:]
            for flow in (0, 1):
                remote(lout.at[flow, j], lin.at[flow, j], leaf_s, leaf_r.at[flow, j], target(flow, 1)).start()
        if own:
            xg[dp, 2 * j - 1, 0:16, :] = rows[0:16]
            ys[2 * j - 1] = rows[16:32]

    def take_leaf(j):
        for flow in (0, 1):
            remote(lin.at[flow, j], lin.at[flow, j], leaf_s, leaf_r.at[flow, j], right).wait_recv()
        a, b = lin[0, j].astype(F32), lin[1, j].astype(F32)
        xg[dp, 2 * j, 0:16, :] = jnp.concatenate([a[0:8], b[0:8]], axis=0).astype(BF16)
        ys[2 * j] = jnp.concatenate([a[8:16], b[8:16]], axis=0).astype(BF16)

    def swap(m):
        return remote(ys.at[pl.ds(2 * m, 2)], xg.at[dp, pl.ds(2 * m, 2), 16:32], y_s, y_r.at[m], ynb)

    def rows_of(d, m):
        return xg.at[d, pl.ds(2 * m, 2)]

    def spread(m):
        swap(m).wait_recv()
        here = rows_of(dp, m)
        remote(here, here, x_s, x_r.at[0, m], x_up).start()
        remote(here, here, x_s, x_r.at[1, m], x_down).start()
        remote(here, here, pc_s, pc_r.at[0, m], core).start()

    def relay(m):
        low, high = rows_of(dp_down, m), rows_of(dp_up, m)
        remote(low, low, x_s, x_r.at[0, m], x_up).wait_recv()
        first = xg.at[dp_down, 2 * m]
        remote(first, first, rel_s, rel_r.at[0, m], x_up).start()
        remote(high, high, x_s, x_r.at[1, m], x_up).wait_recv()
        second = xg.at[dp_up, 2 * m + 1]
        remote(second, second, rel_s, rel_r.at[1, m], x_down).start()
        remote(low, low, pc_s, pc_r.at[1, m], core).start()
        remote(high, high, pc_s, pc_r.at[2, m], core).start()

    def hand_over(m):
        first, second = xg.at[dp_far, 2 * m], xg.at[dp_far, 2 * m + 1]
        remote(first, first, rel_s, rel_r.at[0, m], x_up).wait_recv()
        remote(second, second, rel_s, rel_r.at[1, m], x_up).wait_recv()
        far = rows_of(dp_far, m)
        remote(far, far, pc_s, pc_r.at[3, m], core).start()

    def gathered(m):
        here = rows_of(dp, m)
        for i in range(4):
            remote(here, here, pc_s, pc_r.at[i, m], core).wait_recv()

    for piece in range(CHUNKS):
        for flow in (0, 1):
            ring_send(flow, 0, piece)
    for flow in (0, 1):
        meta_send(flow, 0)
    choose(0, z, z, False, True)

    def ring_step(m, evens, sends):
        for piece in range(CHUNKS):
            for flow in evens:
                ring_wait(flow, m, piece)
                if flow in sends:
                    ring_send(flow, m, piece)
        for flow in evens:
            meta_wait(flow, m)
            if flow in sends:
                meta_send(flow, m)
        last = len(evens) == 1
        choose(m, place(0, 2 * m), z if last else place(1, 2 * m), True, not last)
        take_leaf(m - 1)
        swap(m - 1).start()

    def body(m, carry):
        ring_step(m, (0, 1), (0, 1))
        pl.when(m >= 2)(lambda: spread(m - 2))
        pl.when(m >= 3)(lambda: relay(m - 3))
        pl.when(m >= 4)(lambda: hand_over(m - 4))
        return carry

    sets = half // 2
    lax.fori_loop(1, sets - 1, body, 0)
    ring_step(sets - 1, (0, 1), (0,))
    spread(sets - 3)
    relay(sets - 4)
    hand_over(sets - 5)

    load_gu.wait()
    load_dn.wait()
    span = half // GROUPS
    rows = span * 32
    hidden = guv.shape[1]
    contract = (((1,), (1,)), ((), ()))

    def group_at(g):
        return (GROUPS - 1 - g) * span

    def expand(g):
        p0 = group_at(g)
        gate = up = None
        for d in range(n_dp):
            part_x = xg[d, p0:p0 + span].reshape(rows, width)
            cols = slice(d * width, (d + 1) * width)
            a = lax.dot_general(part_x, guv[0, :, cols], contract, preferred_element_type=F32)
            b = lax.dot_general(part_x, guv[1, :, cols], contract, preferred_element_type=F32)
            gate, up = (a, b) if gate is None else (gate + a, up + b)
        ab[dp, p0 * 32:p0 * 32 + rows, :] = (gate / (1.0 + jnp.exp(-gate)) * up).astype(BF16)
        here = ab.at[dp, p0 * 32:p0 * 32 + rows]
        remote(here, here, ax_s, ax_r.at[0, g], x_up).start()
        remote(here, here, ax_s, ax_r.at[1, g], x_down).start()
        remote(here, here, ap_s, ap_r.at[0, g], core).start()

    def act_relay(g):
        r0 = group_at(g) * 32
        mid, end = r0 + rows // 2, r0 + rows
        low, high = ab.at[dp_down, r0:end], ab.at[dp_up, r0:end]
        remote(low, low, ax_s, ax_r.at[0, g], x_up).wait_recv()
        first = ab.at[dp_down, r0:mid]
        remote(first, first, al_s, al_r.at[0, g], x_up).start()
        remote(low, low, ap_s, ap_r.at[1, g], core).start()
        remote(high, high, ax_s, ax_r.at[1, g], x_up).wait_recv()
        second = ab.at[dp_up, mid:end]
        remote(second, second, al_s, al_r.at[1, g], x_down).start()
        remote(high, high, ap_s, ap_r.at[2, g], core).start()

    def act_hand_over(g):
        r0 = group_at(g) * 32
        mid, end = r0 + rows // 2, r0 + rows
        first, second = ab.at[dp_far, r0:mid], ab.at[dp_far, mid:end]
        remote(first, first, al_s, al_r.at[0, g], x_up).wait_recv()
        remote(second, second, al_s, al_r.at[1, g], x_up).wait_recv()
        far = ab.at[dp_far, r0:end]
        remote(far, far, ap_s, ap_r.at[3, g], core).start()

    def contract_down(g):
        p0 = group_at(g)
        r0 = p0 * 32
        here = ab.at[dp, r0:r0 + rows]
        for i in range(4):
            remote(here, here, ap_s, ap_r.at[i, g], core).wait_recv()
        total = None
        for d in range(n_dp):
            a = jnp.dot(
                ab[d, r0:r0 + rows, :], dnv[d * hidden:(d + 1) * hidden, :], preferred_element_type=F32
            )
            total = a if total is None else total + a
        eo[p0:p0 + span] = total.astype(BF16).reshape(span, 32, width)
        rr[p0:p0 + span, 0:16, :] = eo[p0:p0 + span, 0:16, :]
        remote(
            eo.at[p0:p0 + span, 16:32], rr.at[p0:p0 + span, 16:32], yb_s, yb_r.at[g], ynb
        ).start()

    def swapped(g):
        p0 = group_at(g)
        there = rr.at[p0:p0 + span, 16:32]
        remote(there, there, yb_s, yb_r.at[g], ynb).wait_recv()

    def leaves_send(g):
        for p in range(group_at(g), group_at(g) + span, 2):
            j = p // 2
            res = rr[p].astype(F32)
            bout[0, j] = jnp.concatenate([res[0:8], res[16:24]], axis=0).astype(BF16)
            bout[1, j] = jnp.concatenate([res[8:16], res[24:32]], axis=0).astype(BF16)
            for flow in (0, 1):
                remote(
                    bout.at[flow, j], bin_.at[flow, j], lf_s, lf_r.at[flow, j], target(1 - flow, 1)
                ).start()

    def share(j, own, leaf):
        code = cw[j]
        own_m, other_m, leaf_a, leaf_b = masks(code)
        w, res = (), ()
        if own:
            w += (own_m * code[4:5], other_m * code[5:6])
            res += (rr[2 * j - 1],)
        if leaf:
            for flow in (0, 1):
                remote(bin_.at[flow, j], bin_.at[flow, j], lf_s, lf_r.at[flow, j], left).wait_recv()
            by = jnp.where(first16, code[6:7], code[7:8])
            w += (leaf_a * by, leaf_b * by)
            res += (bin_[0, j], bin_[1, j])
        w = jnp.concatenate(w, axis=0)
        w_high = w.astype(BF16)
        w_low = (w - w_high.astype(F32)).astype(BF16)
        lhs = jnp.concatenate([w_high, w_low], axis=0)
        rhs = jnp.concatenate(res + res, axis=0)
        return lax.dot_general(lhs, rhs, (((0,), (0,)), ((), ())), preferred_element_type=F32)

    def back_wait(flow, j, piece):
        ref = (rbl, rbr)[flow].at[j, pl.ds(piece * part, part)]
        remote(ref, ref, rs_s, rs_r.at[flow, j, piece], left).wait_recv()

    def chain(flow, j, piece, more):
        buf = (rbl, rbr)[flow]
        cut = slice(piece * part, (piece + 1) * part)
        add = ct[flow * tokens + piece * part:flow * tokens + (piece + 1) * part, :]
        if more:
            back_wait(flow, j, piece)
            add = add + buf[j, cut, :].astype(F32)
        buf[j, cut, :] = add.astype(BF16)
        remote(
            buf.at[j, cut], buf.at[j - 1, cut], rs_s, rs_r.at[flow, j - 1, piece], target(1 - flow, 2)
        ).start()

    def back_step(j):
        for piece in range(CHUNKS):
            chain(0, j, piece, j < sets)
            if j < sets:
                chain(1, j, piece, j < sets - 1)

    def back_pair(g):
        j = (GROUPS - g) * span // 2
        swapped(g)
        leaves_send(g)
        ct[...] = share(j, True, g > 0)
        if g == 0:
            oc[...] = ct[tokens:, :] + x_ref[:, mine].astype(F32)
        back_step(j)
        ct[...] = share(j - 1, True, True)
        return j - 1

    ring_step(sets, (0,), ())
    spread(sets - 2)
    relay(sets - 3)
    hand_over(sets - 4)
    gathered(0)
    gathered(1)
    expand(3)
    spread(sets - 1)
    relay(sets - 2)
    hand_over(sets - 3)
    gathered(2)
    gathered(3)
    expand(2)
    relay(sets - 1)
    hand_over(sets - 2)
    act_relay(3)
    gathered(4)
    gathered(5)
    expand(1)
    hand_over(sets - 1)
    act_hand_over(3)
    act_relay(2)
    gathered(6)
    gathered(7)
    expand(0)
    act_relay(1)
    act_hand_over(2)
    contract_down(3)
    act_relay(0)
    act_hand_over(1)
    contract_down(2)
    act_hand_over(0)
    contract_down(1)
    contract_down(0)
    for g in range(GROUPS):
        j = back_pair(g)
        back_step(j)
    ct[...] = share(0, False, True)
    oc[...] = oc[...] + ct[0:tokens, :] + ct[tokens:, :]
    for piece in range(CHUNKS):
        cut = slice(piece * part, (piece + 1) * part)
        back_wait(0, 0, piece)
        back_wait(1, 0, piece)
        fin[cut, :] = (oc[cut, :] + rbl[0, cut, :].astype(F32) + rbr[0, cut, :].astype(F32)).astype(BF16)
    last = remote(fin, out_ref, fin_s, fin_r, over)
    last.start()

    def drained(ref, sem):
        remote(ref, ref, sem, sem, right).wait_send()

    drained(blk.at[0:half - 1], ring_s)
    drained(mt.at[0:half - 1], meta_s)
    drained(lout, leaf_s)
    drained(ys, y_s)
    drained(xg.at[0:2], x_s)
    drained(xg.at[0], rel_s)
    drained(xg.at[0:4], pc_s)
    drained(ab.at[0:2], ax_s)
    drained(ab.at[0], al_s)
    drained(ab.at[0:4], ap_s)
    drained(ys, yb_s)
    drained(blk.at[0:half - 1], rs_s)
    drained(bout, lf_s)
    last.wait()


def body(activations, routes, gate_weights, norm_gain, gate_up_weights, down_weights):
    n_dp, n_exp = lax.axis_size("dp"), lax.axis_size("expert")
    tokens, features = activations.shape[1:]
    hidden = gate_up_weights.shape[2]
    width = features // n_dp
    n_z = n_exp // 2
    half = n_z // 2
    vmem, anywhere = pl.BlockSpec(memory_space=pltpu.VMEM), pl.BlockSpec(memory_space=pl.ANY)
    dma = pltpu.SemaphoreType.DMA
    out = pl.pallas_call(
        functools.partial(kernel, n_dp, n_exp),
        out_shape=jax.ShapeDtypeStruct((tokens, width), BF16),
        in_specs=[vmem, vmem, vmem, vmem, anywhere, anywhere],
        out_specs=vmem,
        scratch_shapes=[
            pltpu.VMEM((2, hidden, features), BF16),
            pltpu.VMEM((hidden * n_dp, width), BF16),
            pltpu.VMEM((n_z, tokens, width), BF16),
            pltpu.VMEM((n_z, 8, 128), F32),
            pltpu.VMEM((half // 2 + 1, 8, 128), F32),
            pltpu.VMEM((128, 128), BF16),
            pltpu.VMEM((half, 16, width), BF16),
            pltpu.VMEM((n_dp, half, 32, width), BF16),
            pltpu.VMEM((n_dp, half * 32, hidden), BF16),
            pltpu.VMEM((half, 32, width), BF16),
            pltpu.VMEM((half, 32, width), BF16),
            pltpu.VMEM((half // 2 + 1, tokens, width), BF16),
            pltpu.VMEM((half // 2, tokens, width), BF16),
            pltpu.VMEM((2 * tokens, width), F32),
            pltpu.VMEM((tokens, width), F32),
            pltpu.VMEM((tokens, width), BF16),
            pltpu.VMEM((2, half // 2, 16, width), BF16),
            pltpu.VMEM((2, half // 2, 16, width), BF16),
            pltpu.VMEM((2, half // 2, 16, width), BF16),
            pltpu.VMEM((2, half // 2, 16, width), BF16),
            dma((2,)),
            dma, dma((2, half // 2, CHUNKS)),
            dma, dma((2, half // 2)),
            dma, dma((2, half // 2)),
            dma, dma((half // 2,)),
            dma, dma((2, half // 2)),
            dma, dma((2, half // 2)),
            dma, dma((4, half // 2)),
            dma, dma((2, GROUPS)),
            dma, dma((2, GROUPS)),
            dma, dma((4, GROUPS)),
            dma, dma((GROUPS,)),
            dma, dma((2, half // 2, CHUNKS)),
            dma, dma((2, half // 2)),
            dma, dma,
        ],
        compiler_params=pltpu.CompilerParams(
            collective_id=0, has_side_effects=True, vmem_limit_bytes=56 * 1024 * 1024
        ),
    )(activations[0], routes[0].T, gate_weights[0].T, norm_gain[None], gate_up_weights[0], down_weights[0])
    return out[None]


def solution(mesh):
    placed = (
        P("section", "expert", None),
        P("section", "expert", None),
        P("section", "expert", None),
        P(),
        P("expert", None, "dp", None),
        P("expert", None, "dp"),
    )
    return jax.shard_map(
        body, mesh=mesh, in_specs=placed, out_specs=P("section", "expert", "dp"), check_vma=False
    )
```

```python
import functools

import jax
import jax.numpy as jnp
from jax import lax
from jax.experimental import pallas as pl
from jax.experimental.pallas import tpu as pltpu
from jax.sharding import PartitionSpec as P

MESH = pl.DeviceIdType.MESH
F32, BF16 = jnp.float32, jnp.bfloat16
CHUNKS = 4
GROUPS = 4


def remote(src, dst, send, recv, device):
    return pltpu.make_async_remote_copy(
        src_ref=src, dst_ref=dst, send_sem=send, recv_sem=recv, device_id=device, device_id_type=MESH
    )


def kernel(
    n_dp, n_exp,
    x_ref, routes_ref, gates_ref, gain_ref, gu_hbm, dn_hbm, out_ref,
    guv, dnv, blk, mt, cw, tri, ys, xg, ab, eo, rr, rbl, rbr, ct, oc, fin, lin, lout, bin_, bout,
    load_sem, ring_s, ring_r, meta_s, meta_r, leaf_s, leaf_r, y_s, y_r, x_s, x_r, rel_s, rel_r, pc_s, pc_r,
    ax_s, ax_r, al_s, al_r, ap_s, ap_r, yb_s, yb_r, rs_s, rs_r, lf_s, lf_r, fin_s, fin_r,
):
    sec, dp, ex = lax.axis_index("section"), lax.axis_index("dp"), lax.axis_index("expert")
    n_z = n_exp // 2
    half = n_z // 2
    z, yl = ex // 2, lax.rem(ex, 2)
    tokens, width = blk.shape[1], blk.shape[2]
    part = tokens // CHUNKS
    right = (sec, dp, lax.rem(ex + 2, n_exp))
    left = (sec, dp, lax.rem(ex + n_exp - 2, n_exp))
    right2 = (sec, dp, lax.rem(ex + 4, n_exp))
    left2 = (sec, dp, lax.rem(ex + n_exp - 4, n_exp))
    ynb = (sec, dp, ex + 1 - 2 * yl)
    dp_up, dp_down = lax.rem(dp + 2, n_dp), lax.rem(dp + n_dp - 2, n_dp)
    dp_far = lax.rem(dp + n_dp // 2, n_dp)
    dp_pc = dp + 1 - 2 * lax.rem(dp, 2)
    x_up, x_down, core = (sec, dp_up, ex), (sec, dp_down, ex), (sec, dp_pc, ex)
    over = (1 - sec, dp, ex)

    barrier = pltpu.get_barrier_semaphore()
    for peer in (right, left, right2, left2, ynb, x_up, x_down, core, over):
        pl.semaphore_signal(barrier, inc=1, device_id=peer, device_id_type=MESH)
    load_gu = pltpu.make_async_copy(gu_hbm, guv, load_sem.at[0])
    load_dn = pltpu.make_async_copy(dn_hbm, dnv, load_sem.at[1])
    load_gu.start()
    load_dn.start()

    wide = x_ref[...].astype(F32)
    scale = lax.rsqrt(jnp.mean(wide * wide, axis=-1, keepdims=True) + 1e-06)
    mine = pl.ds(pl.multiple_of(dp * width, width), width)
    blk[z] = (x_ref[:, mine].astype(F32) * scale * gain_ref[mine].astype(F32)[None]).astype(BF16)
    mt[z, :, 0:64] = routes_ref[...].astype(F32)
    mt[z, :, 64:128] = gates_ref[...]
    a_tok = lax.broadcasted_iota(jnp.int32, (128, 128), 0)
    b_tok = lax.broadcasted_iota(jnp.int32, (128, 128), 1)
    tri[...] = jnp.where((a_tok < b_tok) & ((a_tok < 64) == (b_tok < 64)), 1.0, 0.0).astype(BF16)
    lane = lax.broadcasted_iota(jnp.int32, (8, 128), 1)
    sub = lax.broadcasted_iota(jnp.int32, (8, 128), 0)
    row16 = lax.broadcasted_iota(jnp.int32, (16, 128), 0).astype(F32)
    low16 = lax.broadcasted_iota(jnp.int32, (16, 128), 1) < 64
    first16 = row16 < 8.0
    mate = 1 - 2 * yl
    ahead, behind = lax.rem(ex + 2, n_exp), lax.rem(ex + n_exp - 2, n_exp)
    wanted = (
        jnp.full((8, 128), ex, jnp.int32),
        jnp.full((8, 128), ex + mate, jnp.int32),
        jnp.where(lane < 64, ahead, behind),
        jnp.where(lane < 64, ahead + mate, behind + mate),
    )
    pl.semaphore_wait(barrier, 9)

    def place(flow, k):
        return lax.rem(z + n_z - k, n_z) if flow == 0 else lax.rem(z + k, n_z)

    def target(flow, hops):
        return ((right, right2) if flow == 0 else (left, left2))[hops - 1]

    def ring_send(flow, j, piece):
        ref = blk.at[place(flow, 2 * j), pl.ds(piece * part, part)]
        remote(ref, ref, ring_s, ring_r.at[flow, j, piece], target(flow, 2)).start()

    def ring_wait(flow, j, piece):
        ref = blk.at[place(flow, 2 * j), pl.ds(piece * part, part)]
        remote(ref, ref, ring_s, ring_r.at[flow, j - 1, piece], right).wait_recv()

    def meta_send(flow, j):
        ref = mt.at[place(flow, 2 * j)]
        remote(ref, ref, meta_s, meta_r.at[flow, j], target(flow, 2)).start()

    def meta_wait(flow, j):
        ref = mt.at[place(flow, 2 * j)]
        remote(ref, ref, meta_s, meta_r.at[flow, j - 1], right).wait_recv()

    def masks(code):
        own = jnp.where(code[0:1] == row16, 1.0, 0.0)
        other = jnp.where(code[1:2] == row16, 1.0, 0.0)
        at_a = jnp.where(first16, code[2:3], code[3:4] + 8.0)
        at_b = jnp.where(first16, code[2:3] - 8.0, code[3:4])
        leaf_a = jnp.where((at_a == row16) & low16, 1.0, 0.0)
        leaf_b = jnp.where((at_b == row16) & ~low16, 1.0, 0.0)
        return own, other, leaf_a, leaf_b

    def choose(j, at_a, at_b, own, leaf):
        ma, mb = mt[at_a], mt[at_b]
        named = jnp.where(lane < 64, ma, pltpu.roll(mb, 64, 1))
        weight = jnp.where(lane < 64, pltpu.roll(ma, 64, 1), mb)
        has = weights = jnp.zeros((8, 128), F32)
        for i, expert in enumerate(wanted):
            hit = named == expert.astype(F32)
            has = jnp.where(sub == i, jnp.sum(jnp.where(hit, 1.0, 0.0), axis=0, keepdims=True), has)
            weights = jnp.where(sub == 4 + i, jnp.sum(jnp.where(hit, weight, 0.0), axis=0, keepdims=True), weights)
        rank = jnp.dot(has.astype(BF16), tri[...], preferred_element_type=F32)
        rank = jnp.where(lane < 64, rank, rank + 8.0)
        code = jnp.where(sub < 4, jnp.where(has > 0.5, rank, -100.0), weights)
        cw[j] = code
        mask = masks(code)
        mask = (mask[:2] if own else ()) + (mask[2:] if leaf else ())
        pick = jnp.concatenate(mask, axis=0).astype(BF16)
        both = jnp.concatenate([blk[at_a], blk[at_b]], axis=0)
        rows = jnp.dot(pick, both, preferred_element_type=F32).astype(BF16)
        if leaf:
            lout[0, j] = rows[-32:-16]
            lout[1, j] = rows[-16:]
            for flow in (0, 1):
                remote(lout.at[flow, j], lin.at[flow, j], leaf_s, leaf_r.at[flow, j], target(flow, 1)).start()
        if own:
            xg[dp, 2 * j - 1, 0:16, :] = rows[0:16]
            ys[2 * j - 1] = rows[16:32]

    def take_leaf(j):
        for flow in (0, 1):
            remote(lin.at[flow, j], lin.at[flow, j], leaf_s, leaf_r.at[flow, j], right).wait_recv()
        a, b = lin[0, j].astype(F32), lin[1, j].astype(F32)
        xg[dp, 2 * j, 0:16, :] = jnp.concatenate([a[0:8], b[0:8]], axis=0).astype(BF16)
        ys[2 * j] = jnp.concatenate([a[8:16], b[8:16]], axis=0).astype(BF16)

    def swap(m):
        return remote(ys.at[pl.ds(2 * m, 2)], xg.at[dp, pl.ds(2 * m, 2), 16:32], y_s, y_r.at[m], ynb)

    def rows_of(d, m):
        return xg.at[d, pl.ds(2 * m, 2)]

    def spread(m):
        swap(m).wait_recv()
        here = rows_of(dp, m)
        remote(here, here, x_s, x_r.at[0, m], x_up).start()
        remote(here, here, x_s, x_r.at[1, m], x_down).start()
        remote(here, here, pc_s, pc_r.at[0, m], core).start()

    def relay(m):
        low, high = rows_of(dp_down, m), rows_of(dp_up, m)
        remote(low, low, x_s, x_r.at[0, m], x_up).wait_recv()
        first = xg.at[dp_down, 2 * m]
        remote(first, first, rel_s, rel_r.at[0, m], x_up).start()
        remote(high, high, x_s, x_r.at[1, m], x_up).wait_recv()
        second = xg.at[dp_up, 2 * m + 1]
        remote(second, second, rel_s, rel_r.at[1, m], x_down).start()
        remote(low, low, pc_s, pc_r.at[1, m], core).start()
        remote(high, high, pc_s, pc_r.at[2, m], core).start()

    def hand_over(m):
        first, second = xg.at[dp_far, 2 * m], xg.at[dp_far, 2 * m + 1]
        remote(first, first, rel_s, rel_r.at[0, m], x_up).wait_recv()
        remote(second, second, rel_s, rel_r.at[1, m], x_up).wait_recv()
        far = rows_of(dp_far, m)
        remote(far, far, pc_s, pc_r.at[3, m], core).start()

    def gathered(m):
        here = rows_of(dp, m)
        for i in range(4):
            remote(here, here, pc_s, pc_r.at[i, m], core).wait_recv()

    for piece in range(CHUNKS):
        for flow in (0, 1):
            ring_send(flow, 0, piece)
    for flow in (0, 1):
        meta_send(flow, 0)
    choose(0, z, z, False, True)

    def ring_step(m, evens, sends):
        for piece in range(CHUNKS):
            for flow in evens:
                ring_wait(flow, m, piece)
                if flow in sends:
                    ring_send(flow, m, piece)
        for flow in evens:
            meta_wait(flow, m)
            if flow in sends:
                meta_send(flow, m)
        last = len(evens) == 1
        choose(m, place(0, 2 * m), z if last else place(1, 2 * m), True, not last)
        take_leaf(m - 1)
        swap(m - 1).start()

    def body(m, carry):
        ring_step(m, (0, 1), (0, 1))
        pl.when(m >= 2)(lambda: spread(m - 2))
        pl.when(m >= 3)(lambda: relay(m - 3))
        pl.when(m >= 4)(lambda: hand_over(m - 4))
        return carry

    sets = half // 2
    lax.fori_loop(1, sets - 1, body, 0)
    ring_step(sets - 1, (0, 1), (0,))
    spread(sets - 3)
    relay(sets - 4)
    hand_over(sets - 5)

    load_gu.wait()
    load_dn.wait()
    span = half // GROUPS
    rows = span * 32
    hidden = guv.shape[1]
    contract = (((1,), (1,)), ((), ()))

    def group_at(g):
        return (GROUPS - 1 - g) * span

    def expand(g):
        p0 = group_at(g)
        gate = up = None
        for d in range(n_dp):
            part_x = xg[d, p0:p0 + span].reshape(rows, width)
            cols = slice(d * width, (d + 1) * width)
            a = lax.dot_general(part_x, guv[0, :, cols], contract, preferred_element_type=F32)
            b = lax.dot_general(part_x, guv[1, :, cols], contract, preferred_element_type=F32)
            gate, up = (a, b) if gate is None else (gate + a, up + b)
        ab[dp, p0 * 32:p0 * 32 + rows, :] = (gate / (1.0 + jnp.exp(-gate)) * up).astype(BF16)
        here = ab.at[dp, p0 * 32:p0 * 32 + rows]
        remote(here, here, ax_s, ax_r.at[0, g], x_up).start()
        remote(here, here, ax_s, ax_r.at[1, g], x_down).start()
        remote(here, here, ap_s, ap_r.at[0, g], core).start()

    def act_relay(g):
        r0 = group_at(g) * 32
        mid, end = r0 + rows // 2, r0 + rows
        low, high = ab.at[dp_down, r0:end], ab.at[dp_up, r0:end]
        remote(low, low, ax_s, ax_r.at[0, g], x_up).wait_recv()
        first = ab.at[dp_down, r0:mid]
        remote(first, first, al_s, al_r.at[0, g], x_up).start()
        remote(low, low, ap_s, ap_r.at[1, g], core).start()
        remote(high, high, ax_s, ax_r.at[1, g], x_up).wait_recv()
        second = ab.at[dp_up, mid:end]
        remote(second, second, al_s, al_r.at[1, g], x_down).start()
        remote(high, high, ap_s, ap_r.at[2, g], core).start()

    def act_hand_over(g):
        r0 = group_at(g) * 32
        mid, end = r0 + rows // 2, r0 + rows
        first, second = ab.at[dp_far, r0:mid], ab.at[dp_far, mid:end]
        remote(first, first, al_s, al_r.at[0, g], x_up).wait_recv()
        remote(second, second, al_s, al_r.at[1, g], x_up).wait_recv()
        far = ab.at[dp_far, r0:end]
        remote(far, far, ap_s, ap_r.at[3, g], core).start()

    def contract_down(g):
        p0 = group_at(g)
        r0 = p0 * 32
        here = ab.at[dp, r0:r0 + rows]
        for i in range(4):
            remote(here, here, ap_s, ap_r.at[i, g], core).wait_recv()
        total = None
        for d in range(n_dp):
            a = jnp.dot(
                ab[d, r0:r0 + rows, :], dnv[d * hidden:(d + 1) * hidden, :], preferred_element_type=F32
            )
            total = a if total is None else total + a
        eo[p0:p0 + span] = total.astype(BF16).reshape(span, 32, width)
        rr[p0:p0 + span, 0:16, :] = eo[p0:p0 + span, 0:16, :]
        for at in (1, 0):
            cut = slice(p0 + at * span // 2, p0 + (at + 1) * span // 2)
            remote(eo.at[cut, 16:32], rr.at[cut, 16:32], yb_s, yb_r.at[at, g], ynb).start()

    def swapped(g, at):
        p0 = group_at(g) + at * span // 2
        there = rr.at[p0:p0 + span // 2, 16:32]
        remote(there, there, yb_s, yb_r.at[at, g], ynb).wait_recv()

    def leaves_send(g, at):
        p0 = group_at(g) + at * span // 2
        for p in range(p0, p0 + span // 2, 2):
            j = p // 2
            res = rr[p].astype(F32)
            bout[0, j] = jnp.concatenate([res[0:8], res[16:24]], axis=0).astype(BF16)
            bout[1, j] = jnp.concatenate([res[8:16], res[24:32]], axis=0).astype(BF16)
            for flow in (0, 1):
                remote(
                    bout.at[flow, j], bin_.at[flow, j], lf_s, lf_r.at[flow, j], target(1 - flow, 1)
                ).start()

    def share(j, own, leaf):
        code = cw[j]
        own_m, other_m, leaf_a, leaf_b = masks(code)
        w, res = (), ()
        if own:
            w += (own_m * code[4:5], other_m * code[5:6])
            res += (rr[2 * j - 1],)
        if leaf:
            for flow in (0, 1):
                remote(bin_.at[flow, j], bin_.at[flow, j], lf_s, lf_r.at[flow, j], left).wait_recv()
            by = jnp.where(first16, code[6:7], code[7:8])
            w += (leaf_a * by, leaf_b * by)
            res += (bin_[0, j], bin_[1, j])
        w = jnp.concatenate(w, axis=0)
        w_high = w.astype(BF16)
        w_low = (w - w_high.astype(F32)).astype(BF16)
        lhs = jnp.concatenate([w_high, w_low], axis=0)
        rhs = jnp.concatenate(res + res, axis=0)
        return lax.dot_general(lhs, rhs, (((0,), (0,)), ((), ())), preferred_element_type=F32)

    def back_wait(flow, j, piece):
        ref = (rbl, rbr)[flow].at[j, pl.ds(piece * part, part)]
        remote(ref, ref, rs_s, rs_r.at[flow, j, piece], left).wait_recv()

    def chain(flow, j, piece, more):
        buf = (rbl, rbr)[flow]
        cut = slice(piece * part, (piece + 1) * part)
        add = ct[flow * tokens + piece * part:flow * tokens + (piece + 1) * part, :]
        if more:
            back_wait(flow, j, piece)
            add = add + buf[j, cut, :].astype(F32)
        buf[j, cut, :] = add.astype(BF16)
        remote(
            buf.at[j, cut], buf.at[j - 1, cut], rs_s, rs_r.at[flow, j - 1, piece], target(1 - flow, 2)
        ).start()

    def back_step(j):
        for piece in range(CHUNKS):
            chain(0, j, piece, j < sets)
            if j < sets:
                chain(1, j, piece, j < sets - 1)

    def back_pair(g):
        j = (GROUPS - g) * span // 2
        swapped(g, 1)
        leaves_send(g, 1)
        ct[...] = share(j, True, g > 0)
        if g == 0:
            oc[...] = ct[tokens:, :] + x_ref[:, mine].astype(F32)
        back_step(j)
        swapped(g, 0)
        leaves_send(g, 0)
        ct[...] = share(j - 1, True, True)
        return j - 1

    ring_step(sets, (0,), ())
    spread(sets - 2)
    relay(sets - 3)
    hand_over(sets - 4)
    gathered(0)
    gathered(1)
    expand(3)
    spread(sets - 1)
    relay(sets - 2)
    hand_over(sets - 3)
    gathered(2)
    gathered(3)
    expand(2)
    relay(sets - 1)
    hand_over(sets - 2)
    act_relay(3)
    gathered(4)
    gathered(5)
    expand(1)
    hand_over(sets - 1)
    act_hand_over(3)
    act_relay(2)
    gathered(6)
    gathered(7)
    expand(0)
    act_relay(1)
    act_hand_over(2)
    contract_down(3)
    act_relay(0)
    act_hand_over(1)
    contract_down(2)
    act_hand_over(0)
    contract_down(1)
    contract_down(0)
    for g in range(GROUPS):
        j = back_pair(g)
        back_step(j)
    ct[...] = share(0, False, True)
    oc[...] = oc[...] + ct[0:tokens, :] + ct[tokens:, :]
    for piece in range(CHUNKS):
        cut = slice(piece * part, (piece + 1) * part)
        back_wait(0, 0, piece)
        back_wait(1, 0, piece)
        fin[cut, :] = (oc[cut, :] + rbl[0, cut, :].astype(F32) + rbr[0, cut, :].astype(F32)).astype(BF16)
        remote(fin.at[cut], out_ref.at[cut], fin_s, fin_r.at[piece], over).start()

    def drained(ref, sem):
        remote(ref, ref, sem, sem, right).wait_send()

    drained(blk.at[0:half - 1], ring_s)
    drained(mt.at[0:half - 1], meta_s)
    drained(lout, leaf_s)
    drained(ys, y_s)
    drained(xg.at[0:2], x_s)
    drained(xg.at[0], rel_s)
    drained(xg.at[0:4], pc_s)
    drained(ab.at[0:2], ax_s)
    drained(ab.at[0], al_s)
    drained(ab.at[0:4], ap_s)
    drained(ys, yb_s)
    drained(blk.at[0:half - 1], rs_s)
    drained(bout, lf_s)
    drained(fin, fin_s)
    for piece in range(CHUNKS):
        cut = slice(piece * part, (piece + 1) * part)
        remote(fin.at[cut], out_ref.at[cut], fin_s, fin_r.at[piece], over).wait_recv()


def body(activations, routes, gate_weights, norm_gain, gate_up_weights, down_weights):
    n_dp, n_exp = lax.axis_size("dp"), lax.axis_size("expert")
    tokens, features = activations.shape[1:]
    hidden = gate_up_weights.shape[2]
    width = features // n_dp
    n_z = n_exp // 2
    half = n_z // 2
    vmem, anywhere = pl.BlockSpec(memory_space=pltpu.VMEM), pl.BlockSpec(memory_space=pl.ANY)
    dma = pltpu.SemaphoreType.DMA
    out = pl.pallas_call(
        functools.partial(kernel, n_dp, n_exp),
        out_shape=jax.ShapeDtypeStruct((tokens, width), BF16),
        in_specs=[vmem, vmem, vmem, vmem, anywhere, anywhere],
        out_specs=vmem,
        scratch_shapes=[
            pltpu.VMEM((2, hidden, features), BF16),
            pltpu.VMEM((hidden * n_dp, width), BF16),
            pltpu.VMEM((n_z, tokens, width), BF16),
            pltpu.VMEM((n_z, 8, 128), F32),
            pltpu.VMEM((half // 2 + 1, 8, 128), F32),
            pltpu.VMEM((128, 128), BF16),
            pltpu.VMEM((half, 16, width), BF16),
            pltpu.VMEM((n_dp, half, 32, width), BF16),
            pltpu.VMEM((n_dp, half * 32, hidden), BF16),
            pltpu.VMEM((half, 32, width), BF16),
            pltpu.VMEM((half, 32, width), BF16),
            pltpu.VMEM((half // 2 + 1, tokens, width), BF16),
            pltpu.VMEM((half // 2, tokens, width), BF16),
            pltpu.VMEM((2 * tokens, width), F32),
            pltpu.VMEM((tokens, width), F32),
            pltpu.VMEM((tokens, width), BF16),
            pltpu.VMEM((2, half // 2, 16, width), BF16),
            pltpu.VMEM((2, half // 2, 16, width), BF16),
            pltpu.VMEM((2, half // 2, 16, width), BF16),
            pltpu.VMEM((2, half // 2, 16, width), BF16),
            dma((2,)),
            dma, dma((2, half // 2, CHUNKS)),
            dma, dma((2, half // 2)),
            dma, dma((2, half // 2)),
            dma, dma((half // 2,)),
            dma, dma((2, half // 2)),
            dma, dma((2, half // 2)),
            dma, dma((4, half // 2)),
            dma, dma((2, GROUPS)),
            dma, dma((2, GROUPS)),
            dma, dma((4, GROUPS)),
            dma, dma((2, GROUPS)),
            dma, dma((2, half // 2, CHUNKS)),
            dma, dma((2, half // 2)),
            dma, dma((CHUNKS,)),
        ],
        compiler_params=pltpu.CompilerParams(
            collective_id=0, has_side_effects=True, vmem_limit_bytes=56 * 1024 * 1024
        ),
    )(activations[0], routes[0].T, gate_weights[0].T, norm_gain, gate_up_weights[0], down_weights[0])
    return out[None]


def solution(mesh):
    placed = (
        P("section", "expert", None),
        P("section", "expert", None),
        P("section", "expert", None),
        P(),
        P("expert", None, "dp", None),
        P("expert", None, "dp"),
    )
    return jax.shard_map(
        body, mesh=mesh, in_specs=placed, out_specs=P("section", "expert", "dp"), check_vma=False
    )
```
